32 devices in a mesh: dp: 32 (over z, y, x, core).
Axes of the slice: x: 2, y: 2, z: 4, core: 2. Of those that a mesh axis runs over, the one named last changes fastest.
Arguments:
- hidden_in: bfloat16 [8192, 1024], P('dp'), may hold values from -6 to 6
- seq_lengths: int32 [128], P('dp'), may hold values from 0 to 256, as said below
- qkv_weight: bfloat16 [3072, 1024], P('dp'), may hold values from -0.1875 to 0.1875
- q_bias: bfloat16 [1024], P('dp'), may hold values from -3 to 3
- v_bias: bfloat16 [1024], P('dp'), may hold values from -3 to 3
- out_weight: bfloat16 [1024, 1024], P('dp'), may hold values from -0.75 to 0.75
- out_bias: bfloat16 [1024], P('dp'), may hold values from -3 to 3
- norm1_gain: bfloat16 [1024], P('dp'), may hold values from 0.099609375 to 1.8984375
- norm1_bias: bfloat16 [1024], P('dp'), may hold values from -3 to 3
- up_weight: bfloat16 [4096, 1024], P('dp'), may hold values from -0.1875 to 0.1875
- up_bias: bfloat16 [4096], P('dp'), may hold values from -3 to 3
- down_weight: bfloat16 [1024, 4096], P('dp'), may hold values from -0.09375 to 0.09375
- down_bias: bfloat16 [1024], P('dp'), may hold values from -3 to 3
- norm2_gain: bfloat16 [1024], P('dp'), may hold values from 0.099609375 to 1.8984375
- norm2_bias: bfloat16 [1024], P('dp'), may hold values from -3 to 3
- cotangent: bfloat16 [8192, 1024], P('dp'), may hold values from -6 to 6
Outputs:
- mixed: bfloat16 [8192, 1024], P('dp')
- grad_input: float32 [8192, 1024], P('dp')
- grad_qkv_weight: float32 [3072, 1024], P('dp')
- grad_q_bias: float32 [1024], P('dp')
- grad_v_bias: float32 [1024], P('dp')
- grad_out_weight: float32 [1024, 1024], P('dp')
- grad_out_bias: float32 [1024], P('dp')
- grad_norm1_gain: float32 [1024], P('dp')
- grad_norm1_bias: float32 [1024], P('dp')
- grad_up_weight: float32 [4096, 1024], P('dp')
- grad_up_bias: float32 [4096], P('dp')
- grad_down_weight: float32 [1024, 4096], P('dp')
- grad_down_bias: float32 [1024], P('dp')
- grad_norm2_gain: float32 [1024], P('dp')
- grad_norm2_bias: float32 [1024], P('dp')
The draws below stay inside these ranges and needn't reach their ends.
Inputs may be any that keep to these rules, and one draw needn't show every extreme that they name: seq_lengths[4 * b + j] is the length of the j-th sequence laid in device b's 256 rows, zero for an empty slot; a device's lengths sum to 256 or less, exactly 256 on some device, and some device holds a single sequence of 256 rows.
All inputs are finite; a program needn't handle non-finite values.
Results may differ from the reference program's by a relative error of at most 0.012.
Values may be sent and summed in bfloat16 or wider, within the bound.
No kernel may reach another device: no remote copies, remote signals or barrier semaphores. Data moves between devices by JAX's collectives and lax.ppermute only.
A program may use at most 192 MiB of HBM per device.

```python
import jax
import jax.numpy as jnp
from jax import lax

D = 1024
H = 16
DH = 64
FF = 4096
TOK_DEV = 256
SEQ_DEV = 4
TOKENS = 8192
SEQS = 128


def draw_hidden_in(key, part):
    key_base = jax.random.fold_in(key, 101)
    base = jax.random.normal(key_base, (TOKENS, D), jnp.float32)
    return jnp.clip(base, -6.0, 6.0).astype(jnp.bfloat16)


def draw_seq_lengths(key, part):
    devices = SEQS // SEQ_DEV
    key_fill = jax.random.fold_in(key, 11)
    key_full = jax.random.fold_in(key, 12)
    key_cuts = jax.random.fold_in(key, 13)
    key_long = jax.random.fold_in(key, 14)
    fill = jax.random.randint(key_fill, (devices,), TOK_DEV // 4, TOK_DEV + 1, dtype=jnp.int32)
    full_dev = jax.random.randint(key_full, (), 0, devices, dtype=jnp.int32)
    long_dev = jax.random.randint(key_long, (), 0, devices, dtype=jnp.int32)
    device_ids = jnp.arange(devices, dtype=jnp.int32)
    fill = jnp.where(device_ids == full_dev, TOK_DEV, fill).astype(jnp.int32)
    cuts = jax.random.randint(key_cuts, (devices, SEQ_DEV - 1), 0, TOK_DEV + 1, dtype=jnp.int32)
    cuts = jnp.sort(cuts * fill[:, None] // TOK_DEV, axis=1)
    bounds = jnp.concatenate([jnp.zeros((devices, 1), jnp.int32), cuts, fill[:, None]], axis=1)
    lengths = bounds[:, 1:] - bounds[:, :-1]
    single = jnp.concatenate([jnp.full((devices, 1), TOK_DEV, jnp.int32), jnp.zeros((devices, SEQ_DEV - 1), jnp.int32)], axis=1)
    lengths = jnp.where((device_ids == long_dev)[:, None], single, lengths)
    return lengths.reshape(-1).astype(jnp.int32)


def spiked(drawn, stream_key, source, target, shards_of, factor):
    owner, partner = [(jnp.arange(drawn.shape[axis_at]) // (drawn.shape[axis_at] // shards_of)).reshape([-1 if axis == axis_at else 1 for axis in range(drawn.ndim)]) for axis_at in (source, target)]
    chosen = jax.random.permutation(stream_key, shards_of)[partner]
    strong = (owner == chosen) | (owner == (partner + shards_of // 2) % shards_of)
    return jnp.where(strong, factor * drawn, drawn)


def level_of(rng, shape, split, least, top_value):
    def one(dim, blocks):
        heights = jax.random.uniform(jax.random.fold_in(jax.random.fold_in(rng, 6), dim), (blocks,), jnp.float32, least / len(split), top_value / len(split))
        return jnp.repeat(jnp.exp(heights), shape[dim] // blocks).reshape((-1,) + (1,) * (len(shape) - dim - 1))

    level = one(*split[0])
    for cut in split[1:]:
        level = level * one(*cut)
    return level


def gaussian(rng, extent, deviation, bound, pieces=(), held_as=jnp.bfloat16):
    drawn = deviation * jax.random.normal(rng, extent, jnp.float32)
    if pieces:
        drawn = drawn * level_of(rng, extent, pieces, -0.22, 0.18)
    return jnp.clip(drawn, -bound, bound).astype(held_as)


def noise_with(rng, extent, deviation, bound, split, heavy, held_as=jnp.bfloat16):
    values = deviation * jax.random.normal(rng, extent, jnp.float32)
    if split:
        values = values * level_of(rng, extent, split, -0.22, 0.18)
    return jnp.clip(spiked(values, jax.random.fold_in(rng, 3), *heavy), -bound, bound).astype(held_as)


def setup_inputs(seed: int = 0) -> dict:
    splits = jax.random.split(jax.random.key(seed), 17)
    return {
        "hidden_in": draw_hidden_in(jax.random.fold_in(splits[16], 71), 0),
        "seq_lengths": draw_seq_lengths(jax.random.fold_in(splits[16], 71), 0),
        "qkv_weight": gaussian(splits[2], (3 * D, D), D ** -0.5, 0.1875, ((0, 32),)),
        "q_bias": gaussian(splits[3], (D,), 0.5, 3.0, ((0, 32),)),
        "v_bias": gaussian(splits[4], (D,), 0.5, 3.0, ((0, 32),)),
        "out_weight": gaussian(splits[5], (D, D), (D // 16) ** -0.5, 0.75, ((0, 32),)),
        "out_bias": gaussian(splits[6], (D,), 0.5, 3.0, ((0, 32),)),
        "norm1_gain": jnp.clip(1.0 + 0.18 * jax.random.normal(splits[7], (D,), jnp.float32), 0.099609375, 1.8984375).astype(jnp.bfloat16),
        "norm1_bias": gaussian(splits[8], (D,), 0.5, 3.0, ((0, 32),)),
        "up_weight": gaussian(splits[9], (FF, D), D ** -0.5, 0.1875, ((0, 32),)),
        "up_bias": gaussian(splits[10], (FF,), 0.5, 3.0, ((0, 32),)),
        "down_weight": gaussian(splits[11], (D, FF), FF ** -0.5, 0.09375, ((0, 32),)),
        "down_bias": gaussian(splits[12], (D,), 0.5, 3.0, ((0, 32),)),
        "norm2_gain": jnp.clip(1.0 + 0.18 * jax.random.normal(splits[13], (D,), jnp.float32), 0.099609375, 1.8984375).astype(jnp.bfloat16),
        "norm2_bias": gaussian(splits[14], (D,), 0.5, 3.0, ((0, 32),)),
        "cotangent": noise_with(splits[15], (TOKENS, D), 1.0, 6.0, ((0, 32),), (0, 1, 32, 2.75)),
    }


EPS = 1e-05
NEG = -1e+30
INV_SQRT2 = 0.7071067811865476
INV_SQRT_2PI = 0.3989422804014327

def times_t(left, weight):
    return jnp.dot(left, weight.T, preferred_element_type=jnp.float32)

def t_times(left, right):
    return jnp.dot(left.T, right, preferred_element_type=jnp.float32)

def layer_norm(resid):
    mean = lax.optimization_barrier(jnp.mean(resid, axis=1, keepdims=True))
    cent = resid - mean
    var = lax.optimization_barrier(jnp.mean(cent * cent, axis=1, keepdims=True))
    rstd = lax.rsqrt(var + EPS)
    return (cent * rstd, rstd)

def norm_back(grad, normed, rstd, gain):
    scaled = grad * gain
    return rstd * (scaled - lax.optimization_barrier(jnp.mean(scaled, axis=1, keepdims=True)) - normed * lax.optimization_barrier(jnp.mean(scaled * normed, axis=1, keepdims=True)))

def gelu_grad(preact):
    return 0.5 * (1.0 + lax.erf(preact * INV_SQRT2)) + preact * jnp.exp(-0.5 * preact * preact) * INV_SQRT_2PI

def segments(lengths, rows):
    ends = jnp.cumsum(lengths).astype(jnp.int32)
    position = jnp.arange(rows, dtype=jnp.int32)
    return lax.optimization_barrier(jnp.sum((position[:, None] >= ends[None, :]).astype(jnp.int32), axis=1)).astype(jnp.int32)

def heads(block):
    return block.astype(jnp.float32).reshape(block.shape[0], H, DH)

def scores_of(query, key, allowed):
    score = jnp.einsum('qhd,khd->hqk', heads(query), heads(key)) * DH ** (-0.5)
    return jnp.where(allowed[None], score, NEG)

def layer_block(hidden, cot, lengths, weights):
    wqkv, bq, bv, wo, bo, g1, be1, w1, b1, w2, b2, g2, be2 = weights
    rows = hidden.shape[0]
    segment = segments(lengths, rows)
    valid = (segment < SEQ_DEV).astype(jnp.float32)[:, None]
    allowed = segment[:, None] == segment[None, :]
    joined = times_t(hidden, wqkv)
    query = (joined[:, :D] + bq.astype(jnp.float32)).astype(jnp.bfloat16)
    key = joined[:, D:2 * D].astype(jnp.bfloat16)
    value = (joined[:, 2 * D:] + bv.astype(jnp.float32)).astype(jnp.bfloat16)
    score = scores_of(query, key, allowed)
    top = lax.optimization_barrier(jnp.max(score, axis=2, keepdims=True))
    lse = top + jnp.log(lax.optimization_barrier(jnp.sum(jnp.exp(score - top), axis=2, keepdims=True)))
    prob = jnp.exp(score - lse)
    prob_b = prob.astype(jnp.bfloat16)
    context = jnp.einsum('hqk,khd->qhd', prob_b.astype(jnp.float32), heads(value)).reshape(rows, D).astype(jnp.bfloat16)
    resid1 = times_t(context, wo) + bo.astype(jnp.float32) + hidden.astype(jnp.float32)
    normed1, rstd1 = layer_norm(resid1)
    mid = normed1 * g1.astype(jnp.float32) + be1.astype(jnp.float32)
    mid_b = mid.astype(jnp.bfloat16)
    preact = times_t(mid_b, w1) + b1.astype(jnp.float32)
    act_b = jax.nn.gelu(preact, approximate=False).astype(jnp.bfloat16)
    resid2 = times_t(act_b, w2) + b2.astype(jnp.float32) + mid
    normed2, rstd2 = layer_norm(resid2)
    mixed = ((normed2 * g2.astype(jnp.float32) + be2.astype(jnp.float32)) * valid).astype(jnp.bfloat16)
    grad_out = cot.astype(jnp.float32) * valid
    d_g2 = lax.optimization_barrier(jnp.sum(grad_out * normed2, axis=0))
    d_be2 = lax.optimization_barrier(jnp.sum(grad_out, axis=0))
    grad_r2 = norm_back(grad_out, normed2, rstd2, g2.astype(jnp.float32))
    d_b2 = lax.optimization_barrier(jnp.sum(grad_r2, axis=0))
    grad_r2_b = grad_r2.astype(jnp.bfloat16)
    d_w2 = t_times(grad_r2_b, act_b)
    grad_act = jnp.dot(grad_r2_b, w2, preferred_element_type=jnp.float32)
    grad_pre = grad_act * gelu_grad(preact)
    d_b1 = lax.optimization_barrier(jnp.sum(grad_pre, axis=0))
    grad_pre_b = grad_pre.astype(jnp.bfloat16)
    d_w1 = t_times(grad_pre_b, mid_b)
    grad_mid = jnp.dot(grad_pre_b, w1, preferred_element_type=jnp.float32) + grad_r2
    d_g1 = lax.optimization_barrier(jnp.sum(grad_mid * normed1, axis=0))
    d_be1 = lax.optimization_barrier(jnp.sum(grad_mid, axis=0))
    grad_r1 = norm_back(grad_mid, normed1, rstd1, g1.astype(jnp.float32))
    d_bo = lax.optimization_barrier(jnp.sum(grad_r1, axis=0))
    grad_r1_b = grad_r1.astype(jnp.bfloat16)
    d_wo = t_times(grad_r1_b, context)
    grad_context = jnp.dot(grad_r1_b, wo, preferred_element_type=jnp.float32).astype(jnp.bfloat16)
    grad_ctx_h = heads(grad_context)
    grad_value = jnp.einsum('hqk,qhd->khd', prob_b.astype(jnp.float32), grad_ctx_h)
    grad_prob = jnp.einsum('qhd,khd->hqk', grad_ctx_h, heads(value))
    delta = lax.optimization_barrier(jnp.sum(prob * grad_prob, axis=2, keepdims=True))
    grad_score = (prob * (grad_prob - delta) * DH ** (-0.5)).astype(jnp.bfloat16).astype(jnp.float32)
    grad_query = jnp.einsum('hqk,khd->qhd', grad_score, heads(key)).reshape(rows, D)
    grad_key = jnp.einsum('hqk,qhd->khd', grad_score, heads(query)).reshape(rows, D)
    grad_value = grad_value.reshape(rows, D)
    d_bq = lax.optimization_barrier(jnp.sum(grad_query, axis=0))
    d_bv = lax.optimization_barrier(jnp.sum(grad_value, axis=0))
    grad_joined = jnp.concatenate([grad_query, grad_key, grad_value], axis=1).astype(jnp.bfloat16)
    d_wqkv = t_times(grad_joined, hidden)
    grad_in = jnp.dot(grad_joined, wqkv, preferred_element_type=jnp.float32) + grad_r1
    grads = (d_wqkv, d_bq, d_bv, d_wo, d_bo, d_g1, d_be1, d_w1, d_b1, d_w2, d_b2, d_g2, d_be2)
    return (mixed, grad_in, grads)

def reference(hidden_in, seq_lengths, qkv_weight, q_bias, v_bias, out_weight, out_bias, norm1_gain, norm1_bias, up_weight, up_bias, down_weight, down_bias, norm2_gain, norm2_bias, cotangent):
    blocks = TOKENS // TOK_DEV
    weights = (qkv_weight, q_bias, v_bias, out_weight, out_bias, norm1_gain, norm1_bias, up_weight, up_bias, down_weight, down_bias, norm2_gain, norm2_bias)
    inputs = (hidden_in.reshape(blocks, TOK_DEV, D), cotangent.reshape(blocks, TOK_DEV, D), seq_lengths.reshape(blocks, SEQ_DEV))
    start = tuple((jnp.zeros(w.shape, jnp.float32) for w in weights))

    def step(carry, item):
        mixed, grad_in, grads = layer_block(item[0], item[1], item[2], weights)
        return (tuple((a + b for a, b in zip(carry, grads))), (mixed, grad_in))
    totals, (mixed, grad_in) = lax.scan(step, start, inputs)
    return (mixed.reshape(TOKENS, D), grad_in.reshape(TOKENS, D), totals[0], totals[1], totals[2], totals[3], totals[4], totals[5], totals[6], totals[7], totals[8], totals[9], totals[10], totals[11], totals[12])
```

```python
import jax
import jax.numpy as jnp
from jax import lax
from jax.experimental import pallas as pl
from jax.experimental.pallas import tpu as pltpu
from jax.sharding import PartitionSpec as P

H = 16
DH = 64


EPS = 1e-05
NEG = -1e30
INV_SQRT2 = 0.7071067811865476
INV_SQRT_2PI = 0.3989422804014327


def times_t(left, weight):
    return lax.dot_general(
        left, weight, (((1,), (1,)), ((), ())), preferred_element_type=jnp.float32
    )


def t_times(left, right):
    return lax.dot_general(
        left, right, (((0,), (0,)), ((), ())), preferred_element_type=jnp.float32
    )


def layer_norm(resid):
    mean = jnp.mean(resid, axis=1, keepdims=True)
    cent = resid - mean
    var = jnp.mean(cent * cent, axis=1, keepdims=True)
    rstd = lax.rsqrt(var + EPS)
    return (cent * rstd, rstd)


def norm_back(grad, normed, rstd, gain):
    scaled = grad * gain
    return rstd * (
        scaled
        - jnp.mean(scaled, axis=1, keepdims=True)
        - normed * jnp.mean(scaled * normed, axis=1, keepdims=True)
    )


def gelu_grad(preact):
    return (
        0.5 * (1.0 + lax.erf(preact * INV_SQRT2))
        + preact * jnp.exp(-0.5 * preact * preact) * INV_SQRT_2PI
    )


def heads(block):
    return block.reshape(block.shape[0], H, DH)


def masked_scores(query, key, allowed):
    score = jnp.einsum(
        "qhd,khd->hqk", heads(query), heads(key), preferred_element_type=jnp.float32
    ) * DH ** (-0.5)
    return jnp.where(allowed[None], score, NEG)


def orders_of(n):
    bits = n.bit_length() - 1
    far = list(range(bits - 1, 2, -1))
    return (far + [1, 2, 0], far + [2, 1, 0])


def swap(x, bit, n):
    return lax.ppermute(x, "dp", [(i, i ^ (1 << bit)) for i in range(n)])


def rel_of(position, order):
    rel = 0
    for step, bit in enumerate(order):
        rel |= ((position >> step) & 1) << bit
    return rel


def gather_chain(shard, order, n):
    buf = shard[None]
    for bit in order[:-2]:
        buf = jnp.concatenate([buf, swap(buf, bit, n)], axis=0)
    far = swap(buf, order[-2], n)
    return [buf, far, swap(buf, order[-1], n), swap(far, order[-1], n)]


def add16(a, b):
    return (a.astype(jnp.float32) + b.astype(jnp.float32)).astype(jnp.bfloat16)


def scatter_chain(pieces, order, n):
    got_far = swap(pieces[3], order[-1], n)
    got_near = swap(pieces[2], order[-1], n)
    far = add16(pieces[1], got_far)
    got = swap(far, order[-2], n)
    acc = (pieces[0].astype(jnp.float32) + got_near.astype(jnp.float32)) + got.astype(jnp.float32)
    for bit in reversed(order[:-2]):
        half = acc.shape[0] // 2
        got = swap(acc[half:].astype(jnp.bfloat16), bit, n)
        acc = acc[:half].astype(jnp.bfloat16).astype(jnp.float32) + got.astype(jnp.float32)
    return acc[0]


def place_blocks(me, pieces, orders, rows, cols, n):
    half = cols // 2
    per = n // 4
    count = 8 * per

    def body(me_ref, *refs):
        srcs, out, sems = refs[:8], refs[8], refs[9]
        mine = me_ref[0]
        copies = []
        for color in range(2):
            for part in range(4):
                for p in range(per):
                    rel = rel_of(p + per * part, orders[color])
                    dst = out.at[
                        pl.ds((mine ^ rel) * rows, rows), pl.ds(color * half, half)
                    ]
                    copies.append(
                        pltpu.make_async_copy(
                            srcs[4 * color + part].at[p], dst, sems.at[len(copies)]
                        )
                    )
        for c in copies:
            c.start()
        for c in copies:
            c.wait()

    return pl.pallas_call(
        body,
        out_shape=jax.ShapeDtypeStruct((n * rows, cols), jnp.bfloat16),
        in_specs=[pl.BlockSpec(memory_space=pltpu.SMEM)]
        + [pl.BlockSpec(memory_space=pl.ANY)] * 8,
        out_specs=pl.BlockSpec(memory_space=pl.ANY),
        scratch_shapes=[pltpu.SemaphoreType.DMA((count,))],
        name="place_blocks",
    )(me, *pieces)


def split_blocks(me, grad, orders, rows, cols, n):
    half = cols // 2
    per = n // 4
    count = 8 * per

    def body(me_ref, src, *refs):
        outs, sems = refs[:8], refs[8]
        mine = me_ref[0]
        copies = []
        for color in range(2):
            for part in range(4):
                for p in range(per):
                    rel = rel_of(p + per * part, orders[color])
                    blk = src.at[
                        pl.ds((mine ^ rel) * rows, rows), pl.ds(color * half, half)
                    ]
                    copies.append(
                        pltpu.make_async_copy(
                            blk, outs[4 * color + part].at[p], sems.at[len(copies)]
                        )
                    )
        for c in copies:
            c.start()
        for c in copies:
            c.wait()

    return pl.pallas_call(
        body,
        out_shape=[jax.ShapeDtypeStruct((per, rows, half), jnp.bfloat16)] * 8,
        in_specs=[pl.BlockSpec(memory_space=pltpu.SMEM), pl.BlockSpec(memory_space=pl.ANY)],
        out_specs=[pl.BlockSpec(memory_space=pl.ANY)] * 8,
        scratch_shapes=[pltpu.SemaphoreType.DMA((count,))],
        name="split_blocks",
    )(me, grad)


def per_device(
    n,
    hidden_in,
    seq_lengths,
    qkv_weight,
    q_bias,
    v_bias,
    out_weight,
    out_bias,
    norm1_gain,
    norm1_bias,
    up_weight,
    up_bias,
    down_weight,
    down_bias,
    norm2_gain,
    norm2_bias,
    cotangent,
):
    rows = hidden_in.shape[0]
    width = hidden_in.shape[1]
    orders = orders_of(n)
    bits = n.bit_length() - 1
    me = lax.axis_index("dp").astype(jnp.int32)
    me1 = me.reshape(1)

    def gather_weight(w):
        half = w.shape[1] // 2
        pieces = []
        for color in range(2):
            pieces += gather_chain(w[:, color * half : (color + 1) * half], orders[color], n)
        return pieces

    def place(w, pieces):
        return place_blocks(me1, pieces, orders, w.shape[0], w.shape[1], n)

    def reduce_weight(grad, w):
        pieces = split_blocks(me1, grad.astype(jnp.bfloat16), orders, w.shape[0], w.shape[1], n)
        return jnp.concatenate(
            [scatter_chain(pieces[4 * color : 4 * color + 4], orders[color], n) for color in range(2)],
            axis=1,
        )

    vectors = (q_bias, v_bias, out_bias, norm1_gain, norm1_bias, down_bias, norm2_gain, norm2_bias, up_bias)
    packed = jnp.concatenate(vectors)[None]
    for bit in range(bits):
        packed = jnp.concatenate([packed, swap(packed, bit, n)], axis=0)
    packed = packed[me ^ jnp.arange(n, dtype=jnp.int32)].astype(jnp.float32)
    full = []
    at = 0
    for v in vectors:
        full.append(packed[:, at : at + v.shape[0]].reshape(-1))
        at += v.shape[0]
    bq, bv, bo, g1, be1, b2, g2, be2, b1 = full

    qkv_pieces = gather_weight(qkv_weight)
    out_pieces = gather_weight(out_weight)
    up_pieces = gather_weight(up_weight)
    down_pieces = gather_weight(down_weight)

    ends = jnp.cumsum(seq_lengths)
    position = jnp.arange(rows, dtype=jnp.int32)
    segment = jnp.sum((position[:, None] >= ends[None, :]).astype(jnp.int32), axis=1)
    valid = (segment < seq_lengths.shape[0]).astype(jnp.float32)[:, None]
    allowed = segment[:, None] == segment[None, :]
    wqkv = place(qkv_weight, qkv_pieces)
    joined = times_t(hidden_in, wqkv)
    query = (joined[:, :width] + bq).astype(jnp.bfloat16)
    key = joined[:, width : 2 * width].astype(jnp.bfloat16)
    value = (joined[:, 2 * width :] + bv).astype(jnp.bfloat16)
    score = masked_scores(query, key, allowed)
    top = jnp.max(score, axis=2, keepdims=True)
    lse = top + jnp.log(jnp.sum(jnp.exp(score - top), axis=2, keepdims=True))
    prob_b = jnp.exp(score - lse).astype(jnp.bfloat16)
    context = (
        jnp.einsum("hqk,khd->qhd", prob_b, heads(value), preferred_element_type=jnp.float32)
        .reshape(rows, width)
        .astype(jnp.bfloat16)
    )
    wo = place(out_weight, out_pieces)
    resid1 = times_t(context, wo) + bo + hidden_in.astype(jnp.float32)
    normed1, rstd1 = layer_norm(resid1)
    mid = normed1 * g1 + be1
    mid_b = mid.astype(jnp.bfloat16)
    w1 = place(up_weight, up_pieces)
    preact = times_t(mid_b, w1) + b1
    act_b = jax.nn.gelu(preact, approximate=False).astype(jnp.bfloat16)
    w2 = place(down_weight, down_pieces)
    resid2 = times_t(act_b, w2) + b2 + mid
    normed2, rstd2 = layer_norm(resid2)
    mixed = ((normed2 * g2 + be2) * valid).astype(jnp.bfloat16)
    grad_out = cotangent.astype(jnp.float32) * valid
    d_g2 = jnp.sum(grad_out * normed2, axis=0)
    d_be2 = jnp.sum(grad_out, axis=0)
    grad_r2 = norm_back(grad_out, normed2, rstd2, g2)
    d_b2 = jnp.sum(grad_r2, axis=0)
    grad_r2_b = grad_r2.astype(jnp.bfloat16)
    d_w2 = reduce_weight(t_times(grad_r2_b, act_b), down_weight)
    grad_act = jnp.dot(grad_r2_b, w2, preferred_element_type=jnp.float32)
    grad_pre = grad_act * gelu_grad(preact)
    d_b1 = jnp.sum(grad_pre, axis=0)
    grad_pre_b = grad_pre.astype(jnp.bfloat16)
    d_w1 = reduce_weight(t_times(grad_pre_b, mid_b), up_weight)
    grad_mid = jnp.dot(grad_pre_b, w1, preferred_element_type=jnp.float32) + grad_r2
    d_g1 = jnp.sum(grad_mid * normed1, axis=0)
    d_be1 = jnp.sum(grad_mid, axis=0)
    grad_r1 = norm_back(grad_mid, normed1, rstd1, g1)
    d_bo = jnp.sum(grad_r1, axis=0)
    grad_r1_b = grad_r1.astype(jnp.bfloat16)
    d_wo = reduce_weight(t_times(grad_r1_b, context), out_weight)
    grad_context = jnp.dot(grad_r1_b, wo, preferred_element_type=jnp.float32).astype(
        jnp.bfloat16
    )
    prob = jnp.exp(masked_scores(query, key, allowed) - lse)
    prob_again = prob.astype(jnp.bfloat16)
    grad_ctx_h = heads(grad_context)
    grad_value = jnp.einsum(
        "hqk,qhd->khd", prob_again, grad_ctx_h, preferred_element_type=jnp.float32
    ).reshape(rows, width)
    grad_prob = jnp.einsum(
        "qhd,khd->hqk", grad_ctx_h, heads(value), preferred_element_type=jnp.float32
    )
    delta = jnp.sum(prob * grad_prob, axis=2, keepdims=True)
    grad_score = (prob * (grad_prob - delta) * DH ** (-0.5)).astype(jnp.bfloat16)
    grad_query = jnp.einsum(
        "hqk,khd->qhd", grad_score, heads(key), preferred_element_type=jnp.float32
    ).reshape(rows, width)
    grad_key = jnp.einsum(
        "hqk,qhd->khd", grad_score, heads(query), preferred_element_type=jnp.float32
    ).reshape(rows, width)
    d_bq = jnp.sum(grad_query, axis=0)
    d_bv = jnp.sum(grad_value, axis=0)
    grad_joined = jnp.concatenate([grad_query, grad_key, grad_value], axis=1).astype(jnp.bfloat16)
    d_wqkv = reduce_weight(t_times(grad_joined, hidden_in), qkv_weight)
    grad_input = jnp.dot(grad_joined, wqkv, preferred_element_type=jnp.float32) + grad_r1

    small = jnp.concatenate(
        [g.reshape(n, -1) for g in (d_bq, d_bv, d_bo, d_g1, d_be1, d_b2, d_g2, d_be2, d_b1)], axis=1
    )
    small = small[me ^ jnp.arange(n, dtype=jnp.int32)]
    for bit in reversed(range(bits)):
        half = small.shape[0] // 2
        small = small[:half] + swap(small[half:], bit, n)
    sums = []
    at = 0
    for v in vectors:
        sums.append(small[0, at : at + v.shape[0]])
        at += v.shape[0]
    s_bq, s_bv, s_bo, s_g1, s_be1, s_b2, s_g2, s_be2, s_b1 = sums
    return (
        mixed,
        grad_input,
        d_wqkv,
        s_bq,
        s_bv,
        d_wo,
        s_bo,
        s_g1,
        s_be1,
        d_w1,
        s_b1,
        d_w2,
        s_b2,
        s_g2,
        s_be2,
    )


def solution(mesh):
    n = mesh.shape["dp"]
    mat, vec = P("dp", None), P("dp")
    in_specs = (mat, vec, mat, vec, vec, mat, vec, vec, vec, mat, vec, mat, vec, vec, vec, mat)
    out_specs = (mat, mat, mat, vec, vec, mat, vec, vec, vec, mat, vec, mat, vec, vec, vec)

    def device_program(*args):
        return per_device(n, *args)

    return jax.shard_map(
        device_program, mesh=mesh, in_specs=in_specs, out_specs=out_specs, check_vma=False
    )
```

```python
import jax
import jax.numpy as jnp
from jax import lax
from jax.experimental import pallas as pl
from jax.experimental.pallas import tpu as pltpu
from jax.sharding import PartitionSpec as P

H = 16
DH = 64


EPS = 1e-05
NEG = -1e30
INV_SQRT2 = 0.7071067811865476
INV_SQRT_2PI = 0.3989422804014327
LANES = 128
SCALE = DH ** (-0.5)

F32 = jnp.float32
BF16 = jnp.bfloat16


def nt(a, b):
    return lax.dot_general(a, b, (((1,), (1,)), ((), ())), preferred_element_type=F32)


def nn(a, b):
    return lax.dot_general(a, b, (((1,), (0,)), ((), ())), preferred_element_type=F32)


def tn(a, b):
    return lax.dot_general(a, b, (((0,), (0,)), ((), ())), preferred_element_type=F32)


def layer_norm(resid):
    mean = jnp.mean(resid, axis=1, keepdims=True)
    cent = resid - mean
    var = jnp.mean(cent * cent, axis=1, keepdims=True)
    rstd = lax.rsqrt(var + EPS)
    return (cent * rstd, rstd)


def norm_back(grad, normed, rstd, gain):
    scaled = grad * gain
    return rstd * (
        scaled
        - jnp.mean(scaled, axis=1, keepdims=True)
        - normed * jnp.mean(scaled * normed, axis=1, keepdims=True)
    )


def col_sum(x):
    return jnp.sum(x, axis=0, keepdims=True)


def orders_of(n):
    bits = n.bit_length() - 1
    far = list(range(bits - 1, 2, -1))
    return (far + [1, 2, 0], far + [2, 1, 0])


def swap(x, bit, n):
    return lax.ppermute(x, "dp", [(i, i ^ (1 << bit)) for i in range(n)])


def rel_of(position, order):
    rel = 0
    for step, bit in enumerate(order):
        rel |= ((position >> step) & 1) << bit
    return rel


def gather_far(shard, order, n):
    buf = shard[None]
    for bit in order[:-2]:
        if bit < 3:
            break
        buf = jnp.concatenate([buf, swap(buf, bit, n)], axis=0)
    return buf


def gather_near(buf, order, n):
    for bit in [b for b in order[:-2] if b < 3]:
        buf = jnp.concatenate([buf, swap(buf, bit, n)], axis=0)
    far = swap(buf, order[-2], n)
    return [buf, far, swap(buf, order[-1], n), swap(far, order[-1], n)]


def add16(a, b):
    return (a.astype(F32) + b.astype(F32)).astype(BF16)


def scatter_chain(pieces, order, n):
    got_far = swap(pieces[3], order[-1], n)
    got_near = swap(pieces[2], order[-1], n)
    far = add16(pieces[1], got_far)
    got = swap(far, order[-2], n)
    acc = (pieces[0].astype(F32) + got_near.astype(F32)) + got.astype(F32)
    for bit in reversed(order[:-2]):
        half = acc.shape[0] // 2
        got = swap(acc[half:].astype(BF16), bit, n)
        acc = acc[:half].astype(BF16).astype(F32) + got.astype(F32)
    return acc[0]


class Blocks:
    def __init__(self, n, row0, rows, cols):
        self.n, self.row0, self.rows, self.half = n, row0, rows, cols // 2
        self.shape = (n * rows, cols)

    def each(self, mine):
        per = self.n // 4
        orders = orders_of(self.n)
        for color in range(2):
            for part in range(4):
                for p in range(per):
                    rel = rel_of(p + per * part, orders[color])
                    start = pl.multiple_of((mine ^ rel) * self.rows, self.rows)
                    yield (
                        4 * color + part,
                        (p, pl.ds(self.row0, self.rows)),
                        (pl.ds(start, self.rows), pl.ds(color * self.half, self.half)),
                    )

    def load(self, mine, pieces, full, sem):
        for i, at, to in self.each(mine):
            pltpu.make_async_copy(pieces[i].at[at], full.at[to], sem).start()

    def store(self, mine, full, pieces, sem):
        for i, at, to in self.each(mine):
            pltpu.make_async_copy(full.at[to], pieces[i].at[at], sem).start()

    def wait(self, full, sem):
        pltpu.make_async_copy(full, full, sem).wait()

    def buf(self):
        return pltpu.VMEM(self.shape, BF16)


SMEM = pl.BlockSpec(memory_space=pltpu.SMEM)
ANY = pl.BlockSpec(memory_space=pl.ANY)
VM = pl.BlockSpec(memory_space=pltpu.VMEM)


def shaped(shape, dtype):
    return jax.ShapeDtypeStruct(shape, dtype)


def call(body, name, ins, outs, scratch, flops, args):
    moved = sum(a.size * a.dtype.itemsize for a in args) + sum(
        o.size * o.dtype.itemsize for o, _ in outs
    )
    return pl.pallas_call(
        body,
        out_shape=[o for o, _ in outs],
        in_specs=ins,
        out_specs=[s for _, s in outs],
        scratch_shapes=scratch,
        cost_estimate=pl.CostEstimate(flops=flops, transcendentals=0, bytes_accessed=moved),
        name=name,
    )(*args)


def segments(lens, rows, dim):
    shape = (rows, 1) if dim == 0 else (1, rows)
    pos = lax.broadcasted_iota(jnp.int32, shape, dim)
    seg = jnp.zeros(shape, jnp.int32)
    end = jnp.int32(0)
    for j in range(lens.shape[0]):
        end = end + lens[j]
        seg = seg + (pos >= end).astype(jnp.int32)
    return seg


def lanes_at(i, size):
    return pl.ds(pl.multiple_of(i * size, size), size)


def attn_forward(n, me, lens, h, small, pieces, qkv_rows, out_rows):
    rows, width = h.shape
    wq_b = Blocks(n, 0, qkv_rows, width)
    wo_b = Blocks(n, qkv_rows, out_rows, width)
    chunk = 512

    def body(me_ref, lens_ref, h_ref, small_ref, *refs):
        pieces_r = refs[:8]
        q_ref, k_ref, v_ref, ctx_ref, lse_ref, normed_ref, rstd_ref, midb_ref = refs[8:16]
        wq, wo, mask, sems = refs[16:]
        mine = me_ref[0]
        wq_b.load(mine, pieces_r, wq, sems.at[0])
        wo_b.load(mine, pieces_r, wo, sems.at[1])
        seg_r = segments(lens_ref, rows, 0)
        seg_c = segments(lens_ref, rows, 1)
        mask[...] = (seg_r == seg_c).astype(F32)
        wq_b.wait(wq, sems.at[0])

        for third, (dst, bias) in enumerate(((q_ref, 0), (k_ref, None), (v_ref, 1))):

            def project(i, carry, third=third, dst=dst, bias=bias):
                w = wq[pl.ds(pl.multiple_of(third * width + i * chunk, chunk), chunk), :]
                part = nt(h_ref[...], w)
                if bias is not None:
                    part = part + small_ref[bias : bias + 1, lanes_at(i, chunk)]
                dst[:, lanes_at(i, chunk)] = part.astype(BF16)
                return carry

            lax.fori_loop(0, width // chunk, project, 0)

        def head_group(i, carry):
            at = lanes_at(i, LANES)
            q2, k2, v2 = q_ref[:, at], k_ref[:, at], v_ref[:, at]
            outs, lses = [], []
            for j in range(LANES // DH):
                cut = slice(j * DH, (j + 1) * DH)
                score = nt(q2[:, cut], k2[:, cut]) * SCALE
                score = jnp.where(mask[...] > 0.5, score, NEG)
                top = jnp.max(score, axis=1, keepdims=True)
                e = jnp.exp(score - top)
                total = jnp.sum(e, axis=1, keepdims=True)
                prob = (e * (1.0 / total)).astype(BF16)
                outs.append(nn(prob, v2[:, cut]))
                lses.append(jnp.broadcast_to(top + jnp.log(total), (rows, DH)))
            ctx_ref[:, at] = jnp.concatenate(outs, axis=1).astype(BF16)
            lse_ref[:, at] = jnp.concatenate(lses, axis=1)
            return carry

        lax.fori_loop(0, width // LANES, head_group, 0)
        wo_b.wait(wo, sems.at[1])
        resid = nt(ctx_ref[...], wo[...]) + small_ref[2:3, :] + h_ref[...].astype(F32)
        normed, rstd = layer_norm(resid)
        normed_ref[...] = normed
        rstd_ref[...] = rstd
        midb_ref[...] = (normed * small_ref[3:4, :] + small_ref[4:5, :]).astype(BF16)

    mat16, mat32 = shaped((rows, width), BF16), shaped((rows, width), F32)
    return call(
        body,
        "attn_forward",
        [SMEM, SMEM, VM, VM] + [ANY] * 8,
        [(mat16, VM)] * 4 + [(mat32, VM)] * 2 + [(shaped((rows, 1), F32), VM), (mat16, VM)],
        [wq_b.buf(), wo_b.buf(), pltpu.VMEM((rows, rows), F32), pltpu.SemaphoreType.DMA((2,))],
        9 * rows * width * width,
        (me, lens, h, small, *pieces),
    )


def mlp_up(n, me, mid_b, b1, pieces, up_rows):
    rows, width = mid_b.shape
    w_b = Blocks(n, 0, up_rows, width)
    hidden = w_b.shape[0]
    chunk = 512

    def body(me_ref, mid_ref, b1_ref, *refs):
        pieces_r = refs[:8]
        act_ref, slope_ref, w, sems = refs[8:]
        w_b.load(me_ref[0], pieces_r, w, sems.at[0])
        w_b.wait(w, sems.at[0])

        def step(i, carry):
            at = lanes_at(i, chunk)
            pre = nt(mid_ref[...], w[at, :]) + b1_ref[:, at]
            phi = 0.5 * (1.0 + lax.erf(pre * INV_SQRT2))
            act_ref[:, at] = (pre * phi).astype(BF16)
            slope_ref[:, at] = phi + pre * jnp.exp(-0.5 * pre * pre) * INV_SQRT_2PI
            return carry

        lax.fori_loop(0, hidden // chunk, step, 0)

    return call(
        body,
        "mlp_up",
        [SMEM, VM, VM] + [ANY] * 8,
        [(shaped((rows, hidden), BF16), VM), (shaped((rows, hidden), F32), VM)],
        [w_b.buf(), pltpu.SemaphoreType.DMA((1,))],
        4 * rows * width * hidden,
        (me, mid_b, b1, *pieces),
    )


def mlp_down(n, me, lens, act_b, normed1, small, cot, pieces, down_rows):
    rows, hidden = act_b.shape
    width = normed1.shape[1]
    w_b = Blocks(n, 0, down_rows, hidden)
    per = n // 4

    def body(me_ref, lens_ref, act_ref, n1_ref, small_ref, cot_ref, *refs):
        pieces_r = refs[:8]
        mixed_ref, gr2_ref, gr2b_ref, dg2_ref, dbe2_ref, db2_ref = refs[8:14]
        outs = refs[14:22]
        w, dw, resid_ref, sems = refs[22:]
        mine = me_ref[0]
        w_b.load(mine, pieces_r, w, sems.at[0])
        valid = (segments(lens_ref, rows, 0) < lens_ref.shape[0]).astype(F32)
        w_b.wait(w, sems.at[0])

        def down(i, carry):
            at = lanes_at(i, 256)
            resid_ref[:, at] = nt(act_ref[...], w[at, :])
            return carry

        lax.fori_loop(0, width // 256, down, 0)
        mid = n1_ref[...] * small_ref[3:4, :] + small_ref[4:5, :]
        normed, rstd = layer_norm(resid_ref[...] + small_ref[5:6, :] + mid)
        gain = small_ref[6:7, :]
        mixed_ref[...] = ((normed * gain + small_ref[7:8, :]) * valid).astype(BF16)
        grad_out = cot_ref[...].astype(F32) * valid
        dg2_ref[...] = col_sum(grad_out * normed)
        dbe2_ref[...] = col_sum(grad_out)
        gr2 = norm_back(grad_out, normed, rstd, gain)
        db2_ref[...] = col_sum(gr2)
        gr2_ref[...] = gr2
        gr2b_ref[...] = gr2.astype(BF16)

        def grad(t, carry):
            i, j = t // (hidden // 1024), t % (hidden // 1024)
            left, right = lanes_at(i, 256), lanes_at(j, 1024)
            dw[left, right] = tn(gr2b_ref[:, left], act_ref[:, right]).astype(BF16)
            return carry

        lax.fori_loop(0, (width // 256) * (hidden // 1024), grad, 0)
        w_b.store(mine, dw, outs, sems.at[1])
        w_b.wait(dw, sems.at[1])

    vec = (shaped((1, width), F32), VM)
    return call(
        body,
        "mlp_down",
        [SMEM, SMEM, VM, VM, VM, VM] + [ANY] * 8,
        [(shaped((rows, width), BF16), VM), (shaped((rows, width), F32), VM), (shaped((rows, width), BF16), VM)]
        + [vec] * 3
        + [(shaped((per, down_rows, hidden // 2), BF16), ANY)] * 8,
        [w_b.buf(), w_b.buf(), pltpu.VMEM((rows, width), F32), pltpu.SemaphoreType.DMA((2,))],
        4 * rows * width * hidden,
        (me, lens, act_b, normed1, small, cot, *pieces),
    )


def mlp_up_back(n, me, gr2b, slope, mid_b, pieces, down_rows, up_rows):
    rows, width = gr2b.shape
    hidden = slope.shape[1]
    w_b = Blocks(n, 0, down_rows, hidden)
    d_b = Blocks(n, 0, up_rows, width)
    per = n // 4
    chunk = 512

    def body(me_ref, gr2b_ref, slope_ref, mid_ref, *refs):
        pieces_r = refs[:8]
        gpre_ref, db1_ref = refs[8:10]
        outs = refs[10:18]
        w, dw, sems = refs[18:]
        mine = me_ref[0]
        w_b.load(mine, pieces_r, w, sems.at[0])
        w_b.wait(w, sems.at[0])

        def step(i, carry):
            at = lanes_at(i, chunk)
            g = nn(gr2b_ref[...], w[:, at]) * slope_ref[:, at]
            db1_ref[:, at] = col_sum(g)
            gb = g.astype(BF16)
            gpre_ref[:, at] = gb
            dw[at, :] = tn(gb, mid_ref[...]).astype(BF16)
            return carry

        lax.fori_loop(0, hidden // chunk, step, 0)
        d_b.store(mine, dw, outs, sems.at[1])
        d_b.wait(dw, sems.at[1])

    return call(
        body,
        "mlp_up_back",
        [SMEM, VM, VM, VM] + [ANY] * 8,
        [(shaped((rows, hidden), BF16), VM), (shaped((1, hidden), F32), VM)]
        + [(shaped((per, up_rows, width // 2), BF16), ANY)] * 8,
        [w_b.buf(), d_b.buf(), pltpu.SemaphoreType.DMA((2,))],
        4 * rows * width * hidden,
        (me, gr2b, slope, mid_b, *pieces),
    )


def attn_back(n, me, lens, gpre_b, gr2, normed1, rstd1, small, ctx, q, k, v, lse, h,
              up_pieces, attn_pieces, up_rows, qkv_rows, out_rows):
    rows, width = gr2.shape
    w1_b = Blocks(n, 0, up_rows, width)
    wq_b = Blocks(n, 0, qkv_rows, width)
    wo_b = Blocks(n, qkv_rows, out_rows, width)
    per = n // 4

    def body(me_ref, lens_ref, gpre_ref, gr2_ref, n1_ref, rstd_ref, small_ref, ctx_ref,
             q_ref, k_ref, v_ref, lse_ref, h_ref, *refs):
        ups, attns = refs[:8], refs[8:16]
        gj_ref, gr1_ref, dg1_ref, dbe1_ref, dbo_ref, dbq_ref, dbv_ref = refs[16:23]
        outs = refs[23:31]
        w1, wo, dwo, dwq, gctx, mask, sems = refs[31:]
        mine = me_ref[0]
        w1_b.load(mine, ups, w1, sems.at[0])
        wo_b.load(mine, attns, wo, sems.at[1])
        seg_r = segments(lens_ref, rows, 0)
        seg_c = segments(lens_ref, rows, 1)
        mask[...] = (seg_r == seg_c).astype(F32)
        w1_b.wait(w1, sems.at[0])
        grad_mid = nn(gpre_ref[...], w1[...]) + gr2_ref[...]
        normed = n1_ref[...]
        dg1_ref[...] = col_sum(grad_mid * normed)
        dbe1_ref[...] = col_sum(grad_mid)
        gr1 = norm_back(grad_mid, normed, rstd_ref[...], small_ref[3:4, :])
        dbo_ref[...] = col_sum(gr1)
        gr1_ref[...] = gr1
        gr1_b = gr1.astype(BF16)
        wo_b.wait(wo, sems.at[1])
        gctx[...] = nn(gr1_b, wo[...]).astype(BF16)
        dwo[...] = tn(gr1_b, ctx_ref[...]).astype(BF16)
        wo_b.store(mine, dwo, outs, sems.at[1])

        def head_group(i, carry):
            at = lanes_at(i, LANES)
            q2, k2, v2, g2 = q_ref[:, at], k_ref[:, at], v_ref[:, at], gctx[:, at]
            lse2 = lse_ref[:, at]
            gqs, gks, gvs = [], [], []
            for j in range(LANES // DH):
                cut = slice(j * DH, (j + 1) * DH)
                qh, kh, vh, gh = q2[:, cut], k2[:, cut], v2[:, cut], g2[:, cut]
                score = jnp.where(mask[...] > 0.5, nt(qh, kh) * SCALE, NEG)
                prob = jnp.exp(score - lse2[:, j * DH : j * DH + 1])
                gvs.append(tn(prob.astype(BF16), gh))
                gp = nt(gh, vh)
                delta = jnp.sum(prob * gp, axis=1, keepdims=True)
                gs = (prob * (gp - delta) * SCALE).astype(BF16)
                gqs.append(nn(gs, kh))
                gks.append(tn(gs, qh))
            gq = jnp.concatenate(gqs, axis=1)
            gk = jnp.concatenate(gks, axis=1)
            gv = jnp.concatenate(gvs, axis=1)
            dbq_ref[:, at] = col_sum(gq)
            dbv_ref[:, at] = col_sum(gv)
            gj_ref[:, at] = gq.astype(BF16)
            gj_ref[:, pl.ds(pl.multiple_of(width + i * LANES, LANES), LANES)] = gk.astype(BF16)
            gj_ref[:, pl.ds(pl.multiple_of(2 * width + i * LANES, LANES), LANES)] = gv.astype(BF16)
            return carry

        lax.fori_loop(0, width // LANES, head_group, 0)

        def grad(i, carry):
            at = lanes_at(i, 512)
            dwq[at, :] = tn(gj_ref[:, at], h_ref[...]).astype(BF16)
            return carry

        lax.fori_loop(0, 3 * width // 512, grad, 0)
        wq_b.store(mine, dwq, outs, sems.at[0])
        wo_b.wait(dwo, sems.at[1])
        wq_b.wait(dwq, sems.at[0])

    vec = (shaped((1, width), F32), VM)
    return call(
        body,
        "attn_back",
        [SMEM, SMEM] + [VM] * 11 + [ANY] * 16,
        [(shaped((rows, 3 * width), BF16), VM), (shaped((rows, width), F32), VM)]
        + [vec] * 5
        + [(shaped((per, qkv_rows + out_rows, width // 2), BF16), ANY)] * 8,
        [w1_b.buf(), wo_b.buf(), wo_b.buf(), wq_b.buf(), pltpu.VMEM((rows, width), BF16),
         pltpu.VMEM((rows, rows), F32), pltpu.SemaphoreType.DMA((2,))],
        24 * rows * width * width,
        (me, lens, gpre_b, gr2, normed1, rstd1, small, ctx, q, k, v, lse, h, *up_pieces, *attn_pieces),
    )


def input_grad(n, me, gj, gr1, pieces, qkv_rows):
    rows, width = gr1.shape
    w_b = Blocks(n, 0, qkv_rows, width)

    def body(me_ref, gj_ref, gr1_ref, *refs):
        out_ref, w, sems = refs[8:]
        w_b.load(me_ref[0], refs[:8], w, sems.at[0])
        w_b.wait(w, sems.at[0])
        out_ref[...] = nn(gj_ref[...], w[...]) + gr1_ref[...]

    return call(
        body,
        "input_grad",
        [SMEM, VM, VM] + [ANY] * 8,
        [(shaped((rows, width), F32), VM)],
        [w_b.buf(), pltpu.SemaphoreType.DMA((1,))],
        6 * rows * width * width,
        (me, gj, gr1, *pieces),
    )[0]


PACK_ROWS = 16


def pack_small(vectors, last):
    def body(*refs):
        out = refs[-1]
        out[...] = jnp.zeros_like(out)
        for i, r in enumerate(refs[:-1]):
            out[i : i + 1, : r.shape[1]] = r[...].astype(F32)

    args = [v.reshape(1, -1) for v in vectors] + [last.reshape(1, -1)]
    return call(
        body, "pack_small", [VM] * len(args), [(shaped((PACK_ROWS, LANES), F32), VM)], [], 0, args
    )[0]


def unpack_small(n, me, packed, each, last):
    def body(me_ref, p_ref, vec_ref, last_ref):
        mine = me_ref[0]
        for d in range(n):
            block = p_ref[mine ^ d]
            vec_ref[:, d * each : (d + 1) * each] = block[:8, :each]
            last_ref[:, d * last : (d + 1) * last] = block[8:9, :last]

    return call(
        body,
        "unpack_small",
        [SMEM, VM],
        [(shaped((8, n * each), F32), VM), (shaped((1, n * last), F32), VM)],
        [],
        0,
        (me, packed),
    )


def pack_sums(n, me, vectors, last, each, tail):
    def body(me_ref, *refs):
        out = refs[-1]
        mine = me_ref[0]
        last_ref = refs[-2]
        for d in range(n):
            at = mine ^ d
            for i, r in enumerate(refs[:-2]):
                out[at, i : i + 1, :each] = r[:, d * each : (d + 1) * each]
            out[at, 8:9, :tail] = last_ref[:, d * tail : (d + 1) * tail]

    args = (me, *vectors, last)
    return call(
        body,
        "pack_sums",
        [SMEM] + [VM] * (len(args) - 1),
        [(shaped((n, PACK_ROWS, LANES), F32), VM)],
        [],
        0,
        args,
    )[0]


def after(x, *deps):
    return lax.optimization_barrier((x, *deps))[0]


def per_device(
    n,
    hidden_in,
    seq_lengths,
    qkv_weight,
    q_bias,
    v_bias,
    out_weight,
    out_bias,
    norm1_gain,
    norm1_bias,
    up_weight,
    up_bias,
    down_weight,
    down_bias,
    norm2_gain,
    norm2_bias,
    cotangent,
):
    orders = orders_of(n)
    bits = n.bit_length() - 1
    me = lax.axis_index("dp").astype(jnp.int32).reshape(1)
    qkv_rows, out_rows = qkv_weight.shape[0], out_weight.shape[0]
    up_rows, down_rows = up_weight.shape[0], down_weight.shape[0]

    def color_of(w, color):
        half = w.shape[1] // 2
        return w[:, color * half : (color + 1) * half]

    vectors = (q_bias, v_bias, out_bias, norm1_gain, norm1_bias, down_bias, norm2_gain, norm2_bias)
    each, tail = q_bias.shape[0], up_bias.shape[0]
    packed = pack_small(vectors, up_bias)[None]
    for bit in range(bits):
        packed = jnp.concatenate([packed, swap(packed, bit, n)], axis=0)
    small, b1 = unpack_small(n, me, packed, each, tail)

    attn_far = [
        gather_far(
            jnp.concatenate([color_of(qkv_weight, c), color_of(out_weight, c)], axis=0), orders[c], n
        )
        for c in range(2)
    ]
    up_far = [gather_far(after(color_of(up_weight, c), *attn_far), orders[c], n) for c in range(2)]
    attn_pieces = gather_near(attn_far[0], orders[0], n) + gather_near(attn_far[1], orders[1], n)
    down_far = [gather_far(after(color_of(down_weight, c), *up_far), orders[c], n) for c in range(2)]
    up_pieces = gather_near(up_far[0], orders[0], n) + gather_near(up_far[1], orders[1], n)
    down_pieces = gather_near(down_far[0], orders[0], n) + gather_near(down_far[1], orders[1], n)

    q, k, v, ctx, lse, normed1, rstd1, mid_b = attn_forward(
        n, me, seq_lengths, hidden_in, small, attn_pieces, qkv_rows, out_rows
    )
    act_b, slope = mlp_up(n, me, mid_b, b1, up_pieces, up_rows)
    mixed, gr2, gr2b, d_g2, d_be2, d_b2, *dw2 = mlp_down(
        n, me, seq_lengths, act_b, normed1, small, cotangent, down_pieces, down_rows
    )
    gpre_b, d_b1, *dw1 = mlp_up_back(n, me, gr2b, slope, mid_b, down_pieces, down_rows, up_rows)
    gj, gr1, d_g1, d_be1, d_bo, d_bq, d_bv, *dattn = attn_back(
        n, me, seq_lengths, gpre_b, gr2, normed1, rstd1, small, ctx, q, k, v, lse, hidden_in,
        up_pieces, attn_pieces, up_rows, qkv_rows, out_rows,
    )
    grad_input = input_grad(n, me, gj, gr1, attn_pieces, qkv_rows)

    def reduce(pieces):
        return jnp.concatenate(
            [scatter_chain(pieces[4 * c : 4 * c + 4], orders[c], n) for c in range(2)], axis=1
        )

    down_sum = reduce(dw2)
    up_sum = reduce(dw1)
    attn_sum = reduce(dattn)

    sums = pack_sums(n, me, (d_bq, d_bv, d_bo, d_g1, d_be1, d_b2, d_g2, d_be2), d_b1, each, tail)
    for bit in reversed(range(bits)):
        half = sums.shape[0] // 2
        sums = sums[:half] + swap(sums[half:], bit, n)
    s_bq, s_bv, s_bo, s_g1, s_be1, s_b2, s_g2, s_be2 = [sums[0, i, :each] for i in range(8)]
    s_b1 = sums[0, 8, :tail]
    return (
        mixed,
        grad_input,
        attn_sum[:qkv_rows],
        s_bq,
        s_bv,
        attn_sum[qkv_rows:],
        s_bo,
        s_g1,
        s_be1,
        up_sum,
        s_b1,
        down_sum,
        s_b2,
        s_g2,
        s_be2,
    )


def solution(mesh):
    n = mesh.shape["dp"]
    mat, vec = P("dp", None), P("dp")
    in_specs = (mat, vec, mat, vec, vec, mat, vec, vec, vec, mat, vec, mat, vec, vec, vec, mat)
    out_specs = (mat, mat, mat, vec, vec, mat, vec, vec, vec, mat, vec, mat, vec, vec, vec)

    def device_program(*args):
        return per_device(n, *args)

    return jax.shard_map(
        device_program, mesh=mesh, in_specs=in_specs, out_specs=out_specs, check_vma=False
    )
```

```python
import math

import jax
import jax.numpy as jnp
from jax import lax
from jax.experimental import pallas as pl
from jax.experimental.pallas import tpu as pltpu
from jax.sharding import PartitionSpec as P


DH = 64


EPS = 1e-05
NEG = -1e30
INV_SQRT2 = 0.7071067811865476
INV_SQRT_2PI = 0.3989422804014327
LANES = 128
VMEM_LIMIT = 64 * 2**20 - 65536
SCALE = DH ** (-0.5)

F32 = jnp.float32
BF16 = jnp.bfloat16


def nt(a, b):
    return lax.dot_general(a, b, (((1,), (1,)), ((), ())), preferred_element_type=F32)


def nn(a, b):
    return lax.dot_general(a, b, (((1,), (0,)), ((), ())), preferred_element_type=F32)


def tn(a, b):
    return lax.dot_general(a, b, (((0,), (0,)), ((), ())), preferred_element_type=F32)


def layer_norm(resid):
    mean = jnp.mean(resid, axis=1, keepdims=True)
    cent = resid - mean
    var = jnp.mean(cent * cent, axis=1, keepdims=True)
    rstd = lax.rsqrt(var + EPS)
    return (cent * rstd, rstd)


def norm_back(grad, normed, rstd, gain):
    scaled = grad * gain
    return rstd * (
        scaled
        - jnp.mean(scaled, axis=1, keepdims=True)
        - normed * jnp.mean(scaled * normed, axis=1, keepdims=True)
    )


def col_sum(x):
    return jnp.sum(x, axis=0, keepdims=True)


CHAINS = {"attn": ("abxy", "bayx"), "up": ("bxay", "byax"), "down": ("xyba", "yxab")}


def orders_of(n, group):
    far = list(range(3, n.bit_length() - 1))
    low = far[: len(far) // 2]
    bits = {"x": [1], "y": [2], "a": low, "b": far[len(low) :][::-1]}
    return tuple(tuple(sum((bits[c] for c in chain), []) + [0]) for chain in CHAINS[group])


def swap(x, bit, n):
    return lax.ppermute(x, "dp", [(i, i ^ (1 << bit)) for i in range(n)])


def rel_of(position, order):
    rel = 0
    for step, bit in enumerate(order):
        rel |= ((position >> step) & 1) << bit
    return rel


def gather(shards, group, n):
    orders = orders_of(n, group)
    bufs = [s[None] for s in shards]

    def cross(xs, at):
        return [swap(x, orders[c][at], n) for c, x in enumerate(xs)]

    steps = len(orders[0]) - 2
    for k in range(steps):
        label = steps - k
        got = cross(bufs, k)
        if label > 1:
            bufs = join(bufs, got)
        else:
            bufs = [join(bufs[c : c + 1], got[c : c + 1])[0] for c in range(2)]
    fars = cross(bufs, steps)
    near_c = cross(bufs, -1)
    far_c = cross(fars, -1)
    return sum([[bufs[c], fars[c], near_c[c], far_c[c]] for c in range(2)], [])


def join(firsts, seconds):
    many = len(firsts)

    def body(*refs):
        ins, outs = refs[: 2 * many], refs[2 * many : 3 * many]
        bufs, sems = refs[3 * many : 4 * many], refs[4 * many]
        moves = []
        for i, r in enumerate(ins):
            m = r.shape[0]
            at = pl.ds((i % 2) * m, m)
            buf, out = bufs[i // 2].at[at], outs[i // 2].at[at]
            moves.append(
                (
                    pltpu.make_async_copy(r, buf, sems.at[0, i]),
                    pltpu.make_async_copy(buf, out, sems.at[1, i]),
                )
            )
        for first, _ in moves:
            first.start()
        for first, second in moves:
            first.wait()
            second.start()
        for _, second in moves:
            second.wait()

    args = [x for pair in zip(firsts, seconds) for x in pair]
    shapes = [(2 * a.shape[0],) + a.shape[1:] for a in firsts]
    scratch = [pltpu.VMEM(x, BF16) for x in shapes] + [pltpu.SemaphoreType.DMA((2, 2 * many))]
    outs = [(shaped(x, BF16), ANY) for x in shapes]
    return call(body, [HBM] * (2 * many), outs, scratch, 0, args)


def add_halves(chains):
    many = len(chains)
    blocks = chains[0][0].shape[0]
    step = max(blocks // 4, 1)
    chunks = blocks // step
    order = list(range(chunks // 2, chunks)) + list(range(chunks // 2))

    def body(*refs):
        ins, dst = refs[: 2 * many], refs[2 * many : 4 * many]
        bufs, outs = refs[4 * many : 6 * many], refs[6 * many : 7 * many]
        sems_in, sems_out = refs[7 * many :]
        work = [(c, i) for i in order for c in range(many)]
        loads = {}
        for c, i in work:
            at = pl.ds(i * step, step)
            loads[c, i] = [
                pltpu.make_async_copy(ins[2 * c + k].at[at], bufs[2 * c + k].at[at], sems_in.at[2 * c + k, i])
                for k in range(2)
            ]
            for copy in loads[c, i]:
                copy.start()
        stores = []
        for c, i in work:
            for copy in loads[c, i]:
                copy.wait()
            at = pl.ds(i * step, step)
            outs[c][at] = (bufs[2 * c][at].astype(F32) + bufs[2 * c + 1][at].astype(F32)).astype(BF16)
            to = dst[2 * c + i * step // (blocks // 2)].at[pl.ds(i * step % (blocks // 2), step)]
            stores.append(pltpu.make_async_copy(outs[c].at[at], to, sems_out.at[c, i]))
            stores[-1].start()
        for copy in stores:
            copy.wait()

    args = [p for parts in chains for p in parts]
    out = [(shaped((blocks // 2,) + parts[0].shape[1:], BF16), ANY) for parts in chains for _ in range(2)]
    scratch = [pltpu.VMEM(p.shape, BF16) for p in args] + [pltpu.VMEM(parts[0].shape, BF16) for parts in chains]
    scratch += [pltpu.SemaphoreType.DMA((2 * many, chunks)), pltpu.SemaphoreType.DMA((many, chunks))]
    return call(body, [HBM] * (2 * many), out, scratch, 0, args)


def scatter(pieces, group, n):
    orders = orders_of(n, group)
    keep, send = [pieces[0], pieces[2]], [pieces[1], pieces[3]]
    steps = len(orders[0]) - 1
    for k in range(steps):
        got = [swap(send[c], orders[c][-2 - k], n) for c in range(2)]
        if k == steps - 1:
            return [(keep[c], got[c]) for c in range(2)]
        if k == 0:
            sums = sum([list(add_halves([(keep[c], got[c])])) for c in range(2)], [])
        else:
            sums = add_halves([(keep[c], got[c]) for c in range(2)])
        keep, send = [sums[0], sums[2]], [sums[1], sums[3]]


def finish(chains, cuts):
    parts = [p for c in chains for p in c]
    half = parts[0].shape[2]
    sizes = list(cuts)
    extra = parts[0].shape[1] - sum(sizes)

    def body(*refs):
        ins, outs = refs[: len(parts)], refs[len(parts) :]
        per = len(parts) // 2
        for color in range(2):
            acc = sum(r[0].astype(F32) for r in ins[color * per : (color + 1) * per])
            at = 0
            for o, size in zip(outs, sizes):
                o[:, color * half : (color + 1) * half] = acc[at : at + size]
                at += size
            if extra and color == 0:
                outs[-1][...] = acc[at:]

    outs = [(shaped((size, 2 * half), F32), VM) for size in sizes]
    if extra:
        outs.append((shaped((extra, half), F32), VM))
    return call(body, [VM] * len(parts), outs, [], 0, parts)


class Blocks:
    def __init__(self, n, group, row0, rows, cols):
        self.n, self.row0, self.rows, self.half = n, row0, rows, cols // 2
        self.orders = orders_of(n, group)
        self.shape = (n * rows, cols)

    def each(self, mine):
        per = self.n // 4
        for color in range(2):
            for part in range(4):
                for p in range(per):
                    rel = rel_of(p + per * part, self.orders[color])
                    start = pl.multiple_of((mine ^ rel) * self.rows, self.rows)
                    yield (
                        4 * color + part,
                        (p, pl.ds(self.row0, self.rows)),
                        (pl.ds(start, self.rows), pl.ds(color * self.half, self.half)),
                    )

    def load(self, mine, pieces, full, sems):
        for i, at, to in self.each(mine):
            pltpu.make_async_copy(pieces[i].at[at], full.at[to], sems.at[i // 4]).start()

    def store(self, mine, full, pieces, sems, colors=(0, 1)):
        for i, at, to in self.each(mine):
            if i // 4 in colors:
                pltpu.make_async_copy(full.at[to], pieces[i].at[at], sems.at[i // 4]).start()

    def wait(self, full, sems, colors=(0, 1)):
        for color in colors:
            part = full.at[:, pl.ds(color * self.half, self.half)]
            pltpu.make_async_copy(part, part, sems.at[color]).wait()

    def buf(self):
        return pltpu.VMEM(self.shape, BF16)


SMEM = pl.BlockSpec(memory_space=pltpu.SMEM)
ANY = pl.BlockSpec(memory_space=pl.ANY)
HBM = pl.BlockSpec(memory_space=pltpu.HBM)
VM = pl.BlockSpec(memory_space=pltpu.VMEM)


def shaped(shape, dtype):
    return jax.ShapeDtypeStruct(shape, dtype)


def call(body, ins, outs, scratch, flops, args):
    moved = sum(a.size * a.dtype.itemsize for a in args) + sum(
        o.size * o.dtype.itemsize for o, _ in outs
    )
    return pl.pallas_call(
        body,
        out_shape=[o for o, _ in outs],
        in_specs=ins,
        out_specs=[s for _, s in outs],
        scratch_shapes=scratch,
        cost_estimate=pl.CostEstimate(flops=flops, transcendentals=0, bytes_accessed=moved),
        compiler_params=pltpu.CompilerParams(vmem_limit_bytes=VMEM_LIMIT),
    )(*args)


def segments(lens, rows, dim):
    shape = (rows, 1) if dim == 0 else (1, rows)
    pos = lax.broadcasted_iota(jnp.int32, shape, dim)
    seg = jnp.zeros(shape, jnp.int32)
    end = jnp.int32(0)
    for j in range(lens.shape[0]):
        end = end + lens[j]
        seg = seg + (pos >= end).astype(jnp.int32)
    return seg


def lanes_at(i, size):
    return pl.ds(pl.multiple_of(i * size, size), size)


SMALL = 8


def attn_forward(n, me, lens, h, pieces, qkv_rows, out_rows, each, tail):
    rows, width = h.shape
    per = n // 4
    small_at = qkv_rows + out_rows
    half = width // 2
    wq_b = Blocks(n, "attn", 0, qkv_rows, width)
    wo_b = Blocks(n, "attn", qkv_rows, out_rows, width)
    chunk = 1024

    def body(me_ref, lens_ref, h_ref, *refs):
        pieces_r = refs[:8]
        q_ref, k_ref, v_ref, ctx_ref, lse_ref, normed_ref, rstd_ref, midb_ref = refs[8:16]
        small_ref, tail_ref, wq, wo, mask, tiny, sems = refs[16:]
        mine = me_ref[0]
        for part in range(4):
            for p in range(per):
                rel = rel_of(p + per * part, orders_of(n, "attn")[0])
                pltpu.make_async_copy(
                    pieces_r[part].at[p, pl.ds(small_at, SMALL)], tiny.at[mine ^ rel], sems.at[2, 0]
                ).start()
        wq_b.load(mine, pieces_r, wq, sems.at[0])
        wo_b.load(mine, pieces_r, wo, sems.at[1])
        seg_r = segments(lens_ref, rows, 0)
        seg_c = segments(lens_ref, rows, 1)
        mask[...] = (seg_r == seg_c).astype(F32)
        pltpu.make_async_copy(tiny, tiny, sems.at[2, 0]).wait()
        for d in range(n):
            small_ref[:, d * each : (d + 1) * each] = tiny[d][:, :each].astype(F32)
            tail_ref[:, d * tail : (d + 1) * tail] = tiny[d][:1, LANES : LANES + tail].astype(F32)
        wq_b.wait(wq, sems.at[0])

        for third, (dst, bias) in enumerate(((q_ref, 0), (k_ref, None), (v_ref, 1))):

            def project(i, carry, third=third, dst=dst, bias=bias):
                w = wq[pl.ds(pl.multiple_of(third * width + i * chunk, chunk), chunk), :]
                part = nt(h_ref[...], w)
                if bias is not None:
                    part = part + small_ref[bias : bias + 1, lanes_at(i, chunk)]
                dst[:, lanes_at(i, chunk)] = part.astype(BF16)
                return carry

            lax.fori_loop(0, width // chunk, project, 0)

        def head_group(i, carry):
            at = lanes_at(i, LANES)
            q2, k2, v2 = q_ref[:, at], k_ref[:, at], v_ref[:, at]
            outs, lses = [], []
            for j in range(LANES // DH):
                cut = slice(j * DH, (j + 1) * DH)
                score = nt(q2[:, cut], k2[:, cut]) * SCALE
                score = jnp.where(mask[...] > 0.5, score, NEG)
                top = jnp.max(score, axis=1, keepdims=True)
                e = jnp.exp(score - top)
                total = jnp.sum(e, axis=1, keepdims=True)
                prob = (e * (1.0 / total)).astype(BF16)
                outs.append(nn(prob, v2[:, cut]))
                lses.append(jnp.broadcast_to(top + jnp.log(total), (rows, DH)))
            ctx_ref[:, at] = jnp.concatenate(outs, axis=1).astype(BF16)
            lse_ref[:, at] = jnp.concatenate(lses, axis=1)
            return carry

        lax.fori_loop(0, width // LANES, head_group, 0)
        wo_b.wait(wo, sems.at[1])
        resid = nt(ctx_ref[...], wo[...]) + small_ref[2:3, :] + h_ref[...].astype(F32)
        normed, rstd = layer_norm(resid)
        normed_ref[...] = normed
        rstd_ref[...] = rstd
        midb_ref[...] = (normed * small_ref[3:4, :] + small_ref[4:5, :]).astype(BF16)

    mat16, mat32 = shaped((rows, width), BF16), shaped((rows, width), F32)
    return call(
        body,
        [SMEM, SMEM, VM] + [HBM] * 8,
        [(mat16, VM)] * 4
        + [(mat32, VM)] * 2
        + [(shaped((rows, 1), F32), VM), (mat16, VM)]
        + [(shaped((SMALL, width), F32), VM), (shaped((1, n * tail), F32), VM)],
        [wq_b.buf(), wo_b.buf(), pltpu.VMEM((rows, rows), F32), pltpu.VMEM((n, SMALL, half), BF16),
         pltpu.SemaphoreType.DMA((3, 2))],
        9 * rows * width * width,
        (me, lens, h, *pieces),
    )


def mlp_up(n, me, mid_b, b1, pieces, up_rows):
    rows, width = mid_b.shape
    w_b = Blocks(n, "up", 0, up_rows, width)
    hidden = w_b.shape[0]
    chunk = 1024

    def body(me_ref, mid_ref, b1_ref, *refs):
        pieces_r = refs[:8]
        act_ref, slope_ref, w, sems = refs[8:]
        w_b.load(me_ref[0], pieces_r, w, sems.at[0])
        w_b.wait(w, sems.at[0])

        def step(i, carry):
            at = lanes_at(i, chunk)
            pre = nt(mid_ref[...], w[at, :]) + b1_ref[:, at]
            phi = 0.5 * (1.0 + lax.erf(pre * INV_SQRT2))
            act_ref[:, at] = (pre * phi).astype(BF16)
            slope_ref[:, at] = phi + pre * jnp.exp(-0.5 * pre * pre) * INV_SQRT_2PI
            return carry

        lax.fori_loop(0, hidden // chunk, step, 0)

    return call(
        body,
        [SMEM, VM, VM] + [HBM] * 8,
        [(shaped((rows, hidden), BF16), VM), (shaped((rows, hidden), F32), VM)],
        [w_b.buf(), pltpu.SemaphoreType.DMA((1, 2))],
        4 * rows * width * hidden,
        (me, mid_b, b1, *pieces),
    )


def mlp_down(n, me, lens, act_b, normed1, small, cot, pieces, down_rows):
    rows, hidden = act_b.shape
    width = normed1.shape[1]
    w_b = Blocks(n, "down", 0, down_rows, hidden)

    def body(me_ref, lens_ref, act_ref, n1_ref, small_ref, cot_ref, *refs):
        pieces_r = refs[:8]
        mixed_ref, gr2_ref, gr2b_ref, dg2_ref, dbe2_ref, db2_ref = refs[8:14]
        w, resid_ref, sems = refs[14:]
        mine = me_ref[0]
        w_b.load(mine, pieces_r, w, sems.at[0])
        valid = (segments(lens_ref, rows, 0) < lens_ref.shape[0]).astype(F32)
        mid = n1_ref[...] * small_ref[3:4, :] + small_ref[4:5, :]
        resid_ref[...] = small_ref[5:6, :] + mid
        half = hidden // 2
        for color in range(2):
            w_b.wait(w, sems.at[0], (color,))
            cut = slice(color * half, (color + 1) * half)
            resid_ref[...] += nt(act_ref[:, cut], w[:, cut])
        normed, rstd = layer_norm(resid_ref[...])
        gain = small_ref[6:7, :]
        mixed_ref[...] = ((normed * gain + small_ref[7:8, :]) * valid).astype(BF16)
        grad_out = cot_ref[...].astype(F32) * valid
        dg2_ref[...] = col_sum(grad_out * normed)
        dbe2_ref[...] = col_sum(grad_out)
        gr2 = norm_back(grad_out, normed, rstd, gain)
        db2_ref[...] = col_sum(gr2)
        gr2_ref[...] = gr2
        gr2b_ref[...] = gr2.astype(BF16)

    vec = (shaped((1, width), F32), VM)
    return call(
        body,
        [SMEM, SMEM, VM, VM, VM, VM] + [HBM] * 8,
        [(shaped((rows, width), BF16), VM), (shaped((rows, width), F32), VM), (shaped((rows, width), BF16), VM)]
        + [vec] * 3,
        [w_b.buf(), pltpu.VMEM((rows, width), F32), pltpu.SemaphoreType.DMA((2, 2))],
        2 * rows * width * hidden,
        (me, lens, act_b, normed1, small, cot, *pieces),
    )


class OwnBlocks(Blocks):
    def each(self, mine):
        per = self.n // 4
        for color in range(2):
            for part in range(2):
                for p in range(per):
                    rel = rel_of(p + per * part, self.orders[color])
                    start = pl.multiple_of(((mine ^ rel) >> 1) * self.rows, self.rows)
                    yield (
                        4 * color + part,
                        (p, pl.ds(self.row0, self.rows)),
                        (pl.ds(start, self.rows), pl.ds(color * self.half, self.half)),
                    )

    def buf(self):
        return pltpu.VMEM((self.shape[0] // 2, self.shape[1]), BF16)


def by_color(outs):
    return {0: outs[0], 1: outs[1], 4: outs[2], 5: outs[3]}


def own_columns(mine, rows, refs, dst):
    width = math.lcm(2 * rows, LANES)
    keep = width // 2
    at_row = lax.broadcasted_iota(jnp.int32, (width, keep), 0)
    at_col = lax.broadcasted_iota(jnp.int32, (width, keep), 1)
    source = at_col // rows * (2 * rows) + (mine & 1) * rows + at_col % rows
    one_hot = (at_row == source).astype(F32).astype(BF16)
    for t, ref in enumerate(refs):
        tokens = ref.shape[0]
        for i in range(ref.shape[1] // width):
            got = nn(ref[:, i * width : (i + 1) * width], one_hot)
            dst[t * tokens : (t + 1) * tokens, i * keep : (i + 1) * keep] = got.astype(BF16)


def copy_own_columns(mine, rows, refs, dst, sem):
    copies = []
    for t, ref in enumerate(refs):
        tokens = ref.shape[0]
        for i in range(ref.shape[1] // (2 * rows)):
            source = pl.ds(pl.multiple_of((2 * i + (mine & 1)) * rows, LANES), rows)
            to = dst.at[pl.ds(t * tokens, tokens), pl.ds(i * rows, rows)]
            copies.append(pltpu.make_async_copy(ref.at[:, source], to, sem.at[t]))
            copies[-1].start()
    return copies


def stack_tokens(refs, dst, sem):
    copies = []
    for t, ref in enumerate(refs):
        tokens = ref.shape[0]
        copies.append(pltpu.make_async_copy(ref, dst.at[pl.ds(t * tokens, tokens)], sem.at[t]))
        copies[-1].start()
    return copies


def grad_product(left, right, dst, cols, size=512):
    def step(i, carry):
        up = lanes_at(i, size)
        dst[up, cols] = tn(left[:, up], right[:, cols]).astype(BF16)
        return carry

    lax.fori_loop(0, left.shape[1] // size, step, 0)


def weight_grad(n, me, items, group):
    wide = items[0][1][0].shape[1]
    per = n // 4
    half = wide // 2
    many = len(items)
    shard_rows = sum(r for _, _, r in items)
    blocks, at = [], 0
    for _, _, r in items:
        blocks.append(OwnBlocks(n, group, at, r, wide))
        at += r
    whole = [r % LANES == 0 for _, _, r in items]

    def body(me_ref, *refs):
        ins, outs = refs[: 4 * many], by_color(refs[4 * many : 4 * many + 4])
        left, right, dw = (refs[4 * many + 4 + many * k : 4 * many + 4 + many * (k + 1)] for k in range(3))
        sems = refs[-1]
        mine = me_ref[0]
        copies = []
        for k, (_, _, r) in enumerate(items):
            if whole[k]:
                copies += copy_own_columns(mine, r, ins[4 * k : 4 * k + 2], left[k], sems.at[k, 2])
            copies += stack_tokens(ins[4 * k + 2 : 4 * k + 4], right[k], sems.at[k, 1])
        for k, (_, _, r) in enumerate(items):
            if not whole[k]:
                own_columns(mine, r, ins[4 * k : 4 * k + 2], left[k])
        for c in copies:
            c.wait()
        size = min(half, 1024)
        for color in range(2):
            for k in range(many):
                for start in range(color * half, (color + 1) * half, size):
                    grad_product(left[k], right[k], dw[k], slice(start, start + size))
                blocks[k].store(mine, dw[k], outs, sems.at[k, 0], (color,))
        for k in range(many):
            blocks[k].wait(dw[k], sems.at[k, 0])

    specs, scratch, args = [], [[], [], []], []
    for k, (lefts, rights, r) in enumerate(items):
        rows, height = lefts[0].shape
        specs += [HBM if whole[k] else VM] * 2 + [HBM] * 2
        args += [*lefts, *rights]
        scratch[0].append(pltpu.VMEM((2 * rows, height // 2), BF16))
        scratch[1].append(pltpu.VMEM((2 * rows, wide), BF16))
        scratch[2].append(blocks[k].buf())
    return call(
        body,
        [SMEM] + specs,
        [(shaped((per, shard_rows, half), BF16), ANY)] * 4,
        sum(scratch, []) + [pltpu.SemaphoreType.DMA((many, 3, 2))],
        0,
        (me, *args),
    )


def mlp_slope(n, me, gr2b, slope, pieces, down_rows):
    rows, width = gr2b.shape
    hidden = slope.shape[1]
    w_b = Blocks(n, "down", 0, down_rows, hidden)
    chunk = 1024

    def body(me_ref, gr2b_ref, slope_ref, *refs):
        gpre_ref, db1_ref, w, sems = refs[8:]
        w_b.load(me_ref[0], refs[:8], w, sems.at[0])

        def step(i, carry):
            at = lanes_at(i, chunk)
            g = nn(gr2b_ref[...], w[:, at]) * slope_ref[:, at]
            db1_ref[:, at] = col_sum(g)
            gpre_ref[:, at] = g.astype(BF16)
            return carry

        for color in range(2):
            w_b.wait(w, sems.at[0], (color,))
            lax.fori_loop(color * hidden // (2 * chunk), (color + 1) * hidden // (2 * chunk), step, 0)

    return call(
        body,
        [SMEM, VM, VM] + [HBM] * 8,
        [(shaped((rows, hidden), BF16), VM), (shaped((1, hidden), F32), VM)],
        [w_b.buf(), pltpu.SemaphoreType.DMA((1, 2))],
        2 * rows * width * hidden,
        (me, gr2b, slope, *pieces),
    )


def mid_back(n, me, gpre_b, gr2, normed1, rstd1, small, up_pieces, attn_pieces, up_rows, qkv_rows, out_rows):
    rows, width = gr2.shape
    w1_b = Blocks(n, "up", 0, up_rows, width)
    wo_b = Blocks(n, "attn", qkv_rows, out_rows, width)

    def body(me_ref, gpre_ref, gr2_ref, n1_ref, rstd_ref, small_ref, *refs):
        ups, attns = refs[:8], refs[8:16]
        gr1_ref, gctx_ref, gr1b_ref, dg1_ref, dbe1_ref, dbo_ref = refs[16:22]
        w1, wo, gmid, sems = refs[22:]
        mine = me_ref[0]
        w1_b.load(mine, ups, w1, sems.at[0])
        wo_b.load(mine, attns, wo, sems.at[1])
        half = width // 2
        for color in range(2):
            w1_b.wait(w1, sems.at[0], (color,))
            cut = slice(color * half, (color + 1) * half)
            gmid[:, cut] = nn(gpre_ref[...], w1[:, cut]) + gr2_ref[:, cut]
        grad_mid = gmid[...]
        normed = n1_ref[...]
        dg1_ref[...] = col_sum(grad_mid * normed)
        dbe1_ref[...] = col_sum(grad_mid)
        gr1 = norm_back(grad_mid, normed, rstd_ref[...], small_ref[3:4, :])
        dbo_ref[...] = col_sum(gr1)
        gr1_ref[...] = gr1
        gr1_b = gr1.astype(BF16)
        wo_b.wait(wo, sems.at[1])
        gctx_ref[...] = nn(gr1_b, wo[...]).astype(BF16)
        gr1b_ref[...] = gr1_b

    vec = (shaped((1, width), F32), VM)
    return call(
        body,
        [SMEM] + [VM] * 5 + [HBM] * 16,
        [(shaped((rows, width), F32), VM), (shaped((rows, width), BF16), VM), (shaped((rows, width), BF16), VM)]
        + [vec] * 3,
        [w1_b.buf(), wo_b.buf(), pltpu.VMEM((rows, width), F32), pltpu.SemaphoreType.DMA((2, 2))],
        10 * rows * width * width,
        (me, gpre_b, gr2, normed1, rstd1, small, *up_pieces, *attn_pieces),
    )


def attn_back(lens, gctx, q, k, v, lse, sums, tail_sum):
    rows, width = q.shape
    tail_rows = tail_sum.shape[1] // width
    held = SMALL + (tail_rows + 7) // 8 * 8

    def body(lens_ref, gctx_ref, q_ref, k_ref, v_ref, lse_ref, *refs):
        gj_ref, flat, mask = refs[-3:]
        flat[...] = jnp.zeros_like(flat)
        for i, r in enumerate(refs[: SMALL - 2]):
            flat[i + 2 : i + 3, :] = r[...]
        for i in range(tail_rows):
            flat[SMALL + i : SMALL + i + 1, :] = refs[SMALL - 2][:, i * width : (i + 1) * width]
        seg_r = segments(lens_ref, rows, 0)
        seg_c = segments(lens_ref, rows, 1)
        mask[...] = (seg_r == seg_c).astype(F32)

        def head_group(i, carry):
            at = lanes_at(i, LANES)
            q2, k2, v2, g2 = q_ref[:, at], k_ref[:, at], v_ref[:, at], gctx_ref[:, at]
            lse2 = lse_ref[:, at]
            gqs, gks, gvs = [], [], []
            for j in range(LANES // DH):
                cut = slice(j * DH, (j + 1) * DH)
                qh, kh, vh, gh = q2[:, cut], k2[:, cut], v2[:, cut], g2[:, cut]
                score = jnp.where(mask[...] > 0.5, nt(qh, kh) * SCALE, NEG)
                prob = jnp.exp(score - lse2[:, j * DH : j * DH + 1])
                gvs.append(tn(prob.astype(BF16), gh))
                gp = nt(gh, vh)
                delta = jnp.sum(prob * gp, axis=1, keepdims=True)
                gs = (prob * (gp - delta) * SCALE).astype(BF16)
                gqs.append(nn(gs, kh))
                gks.append(tn(gs, qh))
            gq = jnp.concatenate(gqs, axis=1)
            gk = jnp.concatenate(gks, axis=1)
            gv = jnp.concatenate(gvs, axis=1)
            flat[0:1, at] = col_sum(gq)
            flat[1:2, at] = col_sum(gv)
            gj_ref[:, at] = gq.astype(BF16)
            gj_ref[:, pl.ds(pl.multiple_of(width + i * LANES, LANES), LANES)] = gk.astype(BF16)
            gj_ref[:, pl.ds(pl.multiple_of(2 * width + i * LANES, LANES), LANES)] = gv.astype(BF16)
            return carry

        lax.fori_loop(0, width // LANES, head_group, 0)

    return call(
        body,
        [SMEM] + [VM] * (4 + SMALL),
        [(shaped((rows, 3 * width), BF16), VM), (shaped((held, width), F32), VM)],
        [pltpu.VMEM((rows, rows), F32)],
        12 * rows * rows * width,
        (lens, gctx, q, k, v, lse, *sums, tail_sum),
    )


def attn_weight_grad(n, me, gjs, hs, flats, qkv_rows, each, tail):
    rows, width = hs[0].shape
    wq_b = OwnBlocks(n, "attn", 0, qkv_rows, width)
    per = n // 4
    small_at = qkv_rows
    half = width // 2
    in_row = width // tail

    def body(me_ref, gj0, gj1, f0, f1, h0, h1, *refs):
        outs = by_color(refs[:4])
        gj, h, dwq, flat, tiny, sems = refs[4:]
        mine = me_ref[0]
        copies = stack_tokens((h0, h1), h, sems.at[1])
        flat[...] = f0[...] + f1[...]
        tiny[...] = jnp.zeros_like(tiny)
        for d in range(n):
            tiny[d, :, :each] = flat[:SMALL, d * each : (d + 1) * each].astype(BF16)
            at_row, at_col = SMALL + d // in_row, d % in_row * tail
            tiny[d, :, LANES : LANES + tail] = jnp.broadcast_to(
                flat[at_row : at_row + 1, at_col : at_col + tail], (SMALL, tail)
            ).astype(BF16)
        smalls = []
        for part in range(2):
            for p in range(per):
                rel = rel_of(p + per * part, orders_of(n, "attn")[0])
                smalls.append(
                    pltpu.make_async_copy(
                        tiny.at[mine ^ rel], outs[part].at[p, pl.ds(small_at, SMALL)], sems.at[2, 0]
                    )
                )
                smalls[-1].start()
        own_columns(mine, qkv_rows, (gj0, gj1), gj)
        for c in copies:
            c.wait()
        for color in range(2):
            grad_product(gj, h, dwq, slice(color * half, (color + 1) * half))
            wq_b.store(mine, dwq, outs, sems.at[0], (color,))
        pltpu.make_async_copy(tiny.at[pl.ds(0, n // 2)], tiny.at[pl.ds(0, n // 2)], sems.at[2, 0]).wait()
        wq_b.wait(dwq, sems.at[0])

    def stacked(cols):
        return pltpu.VMEM((2 * rows, cols), BF16)

    return call(
        body,
        [SMEM] + [VM] * 4 + [HBM] * 2,
        [(shaped((per, small_at + SMALL, half), BF16), ANY)] * 2
        + [(shaped((per, small_at, half), BF16), ANY)] * 2,
        [stacked(3 * width // 2), stacked(width), wq_b.buf(),
         pltpu.VMEM(flats[0].shape, F32), pltpu.VMEM((n, SMALL, half), BF16), pltpu.SemaphoreType.DMA((3, 2))],
        6 * rows * width * width,
        (me, *gjs, *flats, *hs),
    )


def input_grad(n, me, gj, gr1, pieces, qkv_rows):
    rows, width = gr1.shape
    w_b = Blocks(n, "attn", 0, qkv_rows, width)

    def body(me_ref, gj_ref, gr1_ref, *refs):
        out_ref, w, sems = refs[8:]
        w_b.load(me_ref[0], refs[:8], w, sems.at[0])
        half = width // 2
        for color in range(2):
            w_b.wait(w, sems.at[0], (color,))
            cut = slice(color * half, (color + 1) * half)
            out_ref[:, cut] = nn(gj_ref[...], w[:, cut]) + gr1_ref[:, cut]

    return call(
        body,
        [SMEM, VM, VM] + [HBM] * 8,
        [(shaped((rows, width), F32), VM)],
        [w_b.buf(), pltpu.SemaphoreType.DMA((1, 2))],
        6 * rows * width * width,
        (me, gj, gr1, *pieces),
    )[0]


def pack(qkv, out, up, down, vectors, last):
    qkv_rows, out_rows = qkv.shape[0], out.shape[0]
    half, wide = qkv.shape[1] // 2, down.shape[1] // 2
    small_at = qkv_rows + out_rows

    def body(qkv_ref, out_ref, up_ref, down_ref, *refs):
        a_ref, b_ref, up0, up1, down0, down1, tiny = refs[-7:]
        for c, ref in enumerate((a_ref, b_ref)):
            ref[:qkv_rows, :] = qkv_ref[:, c * half : (c + 1) * half]
            ref[qkv_rows:small_at, :] = out_ref[:, c * half : (c + 1) * half]
        for c, ref in enumerate((up0, up1)):
            ref[...] = up_ref[:, c * half : (c + 1) * half]
        for c, ref in enumerate((down0, down1)):
            ref[...] = down_ref[:, c * wide : (c + 1) * wide]
        tiny[...] = jnp.zeros_like(tiny)
        for i, r in enumerate(refs[:SMALL]):
            tiny[i : i + 1, : r.shape[1]] = r[...].astype(F32)
        tail = refs[SMALL]
        tiny[0:1, LANES : LANES + tail.shape[1]] = tail[...].astype(F32)
        a_ref[small_at:, :] = tiny[...].astype(BF16)

    args = [qkv, out, up, down] + [v.reshape(1, -1) for v in vectors] + [last.reshape(1, -1)]
    return call(
        body,
        [VM] * len(args),
        [(shaped((small_at + SMALL, half), BF16), VM), (shaped((small_at, half), BF16), VM)]
        + [(shaped((up.shape[0], half), BF16), VM)] * 2
        + [(shaped((down.shape[0], wide), BF16), VM)] * 2,
        [pltpu.VMEM((SMALL, half), F32)],
        0,
        args,
    )


def per_device(
    n,
    hidden_in,
    seq_lengths,
    qkv_weight,
    q_bias,
    v_bias,
    out_weight,
    out_bias,
    norm1_gain,
    norm1_bias,
    up_weight,
    up_bias,
    down_weight,
    down_bias,
    norm2_gain,
    norm2_bias,
    cotangent,
):
    me = lax.axis_index("dp").astype(jnp.int32).reshape(1)
    qkv_rows, out_rows = qkv_weight.shape[0], out_weight.shape[0]
    up_rows, down_rows = up_weight.shape[0], down_weight.shape[0]

    vectors = (q_bias, v_bias, out_bias, norm1_gain, norm1_bias, down_bias, norm2_gain, norm2_bias)
    each, tail = q_bias.shape[0], up_bias.shape[0]
    shards = pack(qkv_weight, out_weight, up_weight, down_weight, vectors, up_bias)

    attn_pieces = gather(shards[:2], "attn", n)
    up_pieces = gather(shards[2:4], "up", n)
    down_pieces = gather(shards[4:], "down", n)

    def both(x):
        return (x, swap(x, 0, n))

    q, k, v, ctx, lse, normed1, rstd1, mid_b, small, b1 = attn_forward(
        n, me, seq_lengths, hidden_in, attn_pieces, qkv_rows, out_rows, each, tail
    )
    act_b, slope = mlp_up(n, me, mid_b, b1, up_pieces, up_rows)
    mixed, gr2, gr2b, d_g2, d_be2, d_b2 = mlp_down(
        n, me, seq_lengths, act_b, normed1, small, cotangent, down_pieces, down_rows
    )

    acts, mids = both(act_b), both(mid_b)
    hs, ctxs = both(hidden_in), both(ctx)
    dw2 = weight_grad(n, me, [(both(gr2b), acts, down_rows)], "down")
    gpre_b, d_b1 = mlp_slope(n, me, gr2b, slope, down_pieces, down_rows)
    gr1, gctx, gr1_b, d_g1, d_be1, d_bo = mid_back(
        n, me, gpre_b, gr2, normed1, rstd1, small, up_pieces, attn_pieces, up_rows, qkv_rows, out_rows
    )
    dw1 = weight_grad(n, me, [(both(gpre_b), mids, up_rows), (both(gr1_b), ctxs, out_rows)], "up")
    gj, flat = attn_back(
        seq_lengths, gctx, q, k, v, lse, (d_bo, d_g1, d_be1, d_b2, d_g2, d_be2), d_b1
    )
    dattn = attn_weight_grad(n, me, both(gj), hs, both(flat), qkv_rows, each, tail)
    grad_input = input_grad(n, me, gj, gr1, attn_pieces, qkv_rows)
    rd, ru, ra = scatter(dw2, "down", n), scatter(dw1, "up", n), scatter(dattn, "attn", n)
    (down_sum,) = finish(rd, [down_rows])
    up_sum, out_sum = finish(ru, [up_rows, out_rows])
    qkv_sum, tiny = finish(ra, [qkv_rows])
    s_bq, s_bv, s_bo, s_g1, s_be1, s_b2, s_g2, s_be2 = [tiny[i, :each] for i in range(SMALL)]
    s_b1 = tiny[0, LANES : LANES + tail]
    return (
        mixed,
        grad_input,
        qkv_sum,
        s_bq,
        s_bv,
        out_sum,
        s_bo,
        s_g1,
        s_be1,
        up_sum,
        s_b1,
        down_sum,
        s_b2,
        s_g2,
        s_be2,
    )


def solution(mesh):
    n = mesh.shape["dp"]
    mat, vec = P("dp", None), P("dp")
    in_specs = (mat, vec, mat, vec, vec, mat, vec, vec, vec, mat, vec, mat, vec, vec, vec, mat)
    out_specs = (mat, mat, mat, vec, vec, mat, vec, vec, vec, mat, vec, mat, vec, vec, vec)

    def device_program(*args):
        return per_device(n, *args)

    return jax.shard_map(
        device_program, mesh=mesh, in_specs=in_specs, out_specs=out_specs, check_vma=False
    )
```
